32 devices in a mesh: ep: 16 (over z, y, core), dp: 2 (over x).
Axes of the slice: x: 2, y: 2, z: 4, core: 2. Of those that a mesh axis runs over, the one named last changes fastest.
Arguments:
- hidden: bfloat16 [2, 1024, 2048], P(None, ('ep', 'dp')), may hold values from -6 to 6
- norm_gain: bfloat16 [2048], replicated, may hold values from 0.5 to 1.5
- gate_weights: float32 [2, 1024, 8], P(None, ('ep', 'dp')), may hold values from 0.05 to 1
- routes: int32 [2, 1024, 8], P(None, ('ep', 'dp')), may hold values from 0 to 15, as said below
- replica_pick: int32 [2, 1024, 8], P(None, ('ep', 'dp')), may hold values from 0 to 1023
- trainer_experts: int32 [16], replicated, may hold values from 0 to 15, each once
- hot_experts: int32 [3], replicated, may hold values from 0 to 15, as said below
- replica_hot: int32 [16], replicated, may hold values from 0 to 2, as said below
- w_gate: bfloat16 [16, 2048, 384], P('ep', 'dp'), may hold values from -0.125 to 0.125
- w_up: bfloat16 [16, 2048, 384], P('ep', 'dp'), may hold values from -0.125 to 0.125
- w_down: bfloat16 [16, 384, 2048], P('ep', None, 'dp'), may hold values from -0.3125 to 0.3125
- queries: bfloat16 [2, 1024, 4096], P(None, ('ep', 'dp')), may hold values from -6 to 6
- key_cache: bfloat16 [1024, 32, 512], P(('ep', 'dp')), may hold values from -6 to 6
- value_cache: bfloat16 [1024, 32, 512], P(('ep', 'dp')), may hold values from -6 to 6
- new_keys: bfloat16 [2, 1024, 512], P(None, ('ep', 'dp')), may hold values from -6 to 6
- new_values: bfloat16 [2, 1024, 512], P(None, ('ep', 'dp')), may hold values from -6 to 6
- cache_lengths: int32 [1024], P(('ep', 'dp')), may hold values from 2 to 32, as said below
Outputs:
- mixed: bfloat16 [2, 1024, 2048], P(None, ('ep', 'dp'))
- context: bfloat16 [2, 1024, 4096], P(None, ('ep', 'dp'))
The draws below stay inside these ranges and needn't reach their ends.
Inputs may be any that keep to these rules, and one draw needn't show every extreme that they name: Trainer index p holds expert trainer_experts[p]; each expert once. `hot_experts`: 3 different experts, among them expert 0 and expert 16 - 1. `replica_hot`: every entry of hot_experts is named by some index. `cache_lengths`: the 32 sequences of each device include one with 32 live entries. `routes`: each row names 8 different experts; every expert is named by some row.
All inputs are finite; a program needn't handle non-finite values.
Results may differ from the reference program's by a relative error of at most 0.001.
The reference program's roundings to bfloat16 on the way count: a program that leaves them out, or rounds other values in their place, can miss the bound.
Values may be sent and summed in bfloat16 or wider, within the bound.
No kernel may reach another device: no remote copies, remote signals or barrier semaphores. Data moves between devices by JAX's collectives and lax.ppermute only.
A program may use at most 64 MiB of HBM per device.

```python
import math
import jax
import jax.numpy as jnp
from jax import lax

D = 2048
FF = 384
HEADS = 32
KV_HEADS = 4
HEAD = 128
TOP = 8
CAP = 3
SLOTS = 2
HOT = 3
STEPS = 2
TOK_DEV = 32
CACHE = 32
EXPERTS = 16
TOKENS = 1024
N_EP = 16


def hot_choice(key):
    picked = jax.random.permutation(jax.random.fold_in(key, 3), EXPERTS)[:HOT].astype(jnp.int32)
    largest = jnp.max(picked)
    picked = jnp.where(picked == largest, EXPERTS - 1, picked)
    smallest = jnp.min(picked)
    picked = jnp.where(picked == smallest, 0, picked)
    return picked.astype(jnp.int32)


def draw_hot_experts(key, part):
    return hot_choice(key)


def draw_routes(key, part):
    hot_ids = hot_choice(key)
    expert_ids = jnp.arange(EXPERTS, dtype=jnp.int32)
    hot_mask = jnp.sum((expert_ids[:, None] == hot_ids[None, :]).astype(jnp.int32), axis=1)
    base_scores = jax.random.randint(jax.random.fold_in(key, 21), (STEPS, TOKENS, EXPERTS), 0, 65536)
    lucky = (jax.random.randint(jax.random.fold_in(key, 22), (STEPS, TOKENS, EXPERTS), 0, 10) < 9).astype(jnp.int32)
    scores = (base_scores + hot_mask[None, None, :] * lucky * 65536) * EXPERTS + expert_ids[None, None, :]
    return jax.lax.top_k(scores.astype(jnp.int32), TOP)[1].astype(jnp.int32)


def draw_replica_hot(key, part):
    base_key = jax.random.fold_in(key, 4)
    keys_four = jax.random.split(base_key, 4)
    factor_one = jax.random.randint(keys_four[0], (EXPERTS,), 0, HOT)
    factor_two = jax.random.randint(keys_four[1], (EXPERTS,), 0, HOT)
    skewed = factor_one * factor_two // HOT
    position = jnp.arange(EXPERTS)
    skewed = jnp.where(position < HOT, position, skewed)
    relabel = jax.random.permutation(keys_four[2], HOT)
    labelled = relabel[skewed]
    return labelled[jax.random.permutation(keys_four[3], EXPERTS)].astype(jnp.int32)


def draw_cache_lengths(key, part):
    lengths = jax.random.randint(jax.random.fold_in(key, 5), (TOKENS,), 2, CACHE + 1)
    block_pick = jax.random.randint(jax.random.fold_in(key, 6), (TOKENS // TOK_DEV,), 0, TOK_DEV)
    longest = jnp.repeat(block_pick, TOK_DEV) == jnp.arange(TOKENS) % TOK_DEV
    return jnp.where(longest, CACHE, lengths).astype(jnp.int32)


def draw_key_cache(key, part):
    noise = jnp.clip(jax.random.normal(jax.random.fold_in(key, 11), (TOKENS, CACHE, KV_HEADS * HEAD), jnp.float32), -6.0, 6.0)
    return noise.astype(jnp.bfloat16)


def draw_queries(key, part):
    noise = jnp.clip(jax.random.normal(jax.random.fold_in(key, 13), (STEPS, TOKENS, HEADS * HEAD), jnp.float32), -6.0, 6.0)
    return noise.astype(jnp.bfloat16)


def set_ends(drawn, rng, low, high):
    place = [jax.random.randint(jax.random.fold_in(rng, axis), (), 0, length) for axis, length in enumerate(drawn.shape)]
    widest = drawn.shape.index(max(drawn.shape))
    beside = place[:widest] + [(place[widest] + 1) % drawn.shape[widest]] + place[widest + 1:]
    return drawn.at[tuple(place)].set(low).at[tuple(beside)].set(high)


def shard_levels(own_key, shape, cuts, low, top_value):
    def one(dim, blocks):
        heights = jax.random.uniform(jax.random.fold_in(jax.random.fold_in(own_key, 6), dim), (blocks,), jnp.float32, low / len(cuts), top_value / len(cuts))
        return jnp.repeat(jnp.exp(heights), shape[dim] // blocks).reshape((-1,) + (1,) * (len(shape) - dim - 1))

    gain = one(*cuts[0])
    for cut in cuts[1:]:
        gain = gain * one(*cut)
    return gain


def scatter_about(rng, extent, scale, reach, cuts=(), kind=jnp.bfloat16):
    drawn = scale * jax.random.normal(rng, extent, jnp.float32)
    if cuts:
        drawn = drawn * shard_levels(rng, extent, cuts, -0.22, 0.18)
    return jnp.clip(drawn, -reach, reach).astype(kind)


def setup_inputs(seed: int = 0) -> dict:
    seeds = jax.random.split(jax.random.key(seed), 18)
    return {
        "hidden": scatter_about(seeds[0], (STEPS, TOKENS, D), 1.0, 6.0, ((1, 32),)),
        "norm_gain": jnp.clip(1.0 + 0.1 * jax.random.normal(seeds[1], (D,), jnp.float32), 0.5, 1.5).astype(jnp.bfloat16),
        "gate_weights": jnp.clip(jnp.exp(math.log(1.0) - 2.9957323 * jax.random.uniform(seeds[2], (STEPS, TOKENS, TOP), jnp.float32) ** shard_levels(seeds[2], (STEPS, TOKENS, TOP), ((1, 32),), -0.2, 0.2)), 0.05, 1.0),
        "routes": draw_routes(jax.random.fold_in(seeds[17], 71), 0),
        "replica_pick": set_ends(jax.random.randint(seeds[4], (STEPS, TOKENS, TOP), 0, 64 * EXPERTS), jax.random.fold_in(seeds[4], 1), 0, (64 * EXPERTS) - 1).astype(jnp.int32),
        "trainer_experts": jax.random.permutation(seeds[5], EXPERTS).astype(jnp.int32),
        "hot_experts": draw_hot_experts(jax.random.fold_in(seeds[17], 71), 0),
        "replica_hot": draw_replica_hot(jax.random.fold_in(seeds[17], 71), 0),
        "w_gate": scatter_about(seeds[8], (EXPERTS, D, FF), D ** -0.5, 0.125, ((0, 16), (1, 2))),
        "w_up": scatter_about(seeds[9], (EXPERTS, D, FF), D ** -0.5, 0.125, ((0, 16), (1, 2))),
        "w_down": scatter_about(seeds[10], (EXPERTS, FF, D), FF ** -0.5, 0.3125, ((0, 16), (2, 2))),
        "queries": draw_queries(jax.random.fold_in(seeds[17], 71), 0),
        "key_cache": draw_key_cache(jax.random.fold_in(seeds[17], 71), 0),
        "value_cache": scatter_about(seeds[13], (TOKENS, CACHE, KV_HEADS * HEAD), 1.0, 6.0, ((0, 32),)),
        "new_keys": scatter_about(seeds[14], (STEPS, TOKENS, KV_HEADS * HEAD), 1.0, 6.0, ((1, 32),)),
        "new_values": scatter_about(seeds[15], (STEPS, TOKENS, KV_HEADS * HEAD), 1.0, 6.0, ((1, 32),)),
        "cache_lengths": draw_cache_lengths(jax.random.fold_in(seeds[17], 71), 0),
    }


norm_epsilon = 1e-06

def scaled_norm(hidden_rows, norm_gain):
    values = hidden_rows.astype(jnp.float32)
    mean_square = lax.optimization_barrier(jnp.mean(values * values, axis=-1, keepdims=True))
    return (values * lax.rsqrt(mean_square + norm_epsilon) * norm_gain.astype(jnp.float32)).astype(jnp.bfloat16)

def attend_block(inputs, step_index):
    query_rows, cached_keys, cached_values, fresh_keys, fresh_values, lengths = inputs
    rows_here = query_rows.shape[0]
    grouped = query_rows.astype(jnp.float32).reshape(rows_here, KV_HEADS, HEADS // KV_HEADS, HEAD)
    keys_cached = cached_keys.astype(jnp.float32).reshape(rows_here, CACHE, KV_HEADS, HEAD)
    values_cached = cached_values.astype(jnp.float32).reshape(rows_here, CACHE, KV_HEADS, HEAD)
    keys_fresh = fresh_keys.astype(jnp.float32).reshape(rows_here, STEPS, KV_HEADS, HEAD)
    values_fresh = fresh_values.astype(jnp.float32).reshape(rows_here, STEPS, KV_HEADS, HEAD)
    score_scale = 1.0 / math.sqrt(HEAD)
    cache_scores = jnp.einsum('rkgh,rckh->rkgc', grouped, keys_cached) * score_scale
    fresh_scores = jnp.einsum('rkgh,rskh->rkgs', grouped, keys_fresh) * score_scale
    cache_mask = (jnp.arange(CACHE, dtype=jnp.int32)[None, :] < lengths[:, None])[:, None, None, :]
    fresh_mask = (jnp.arange(STEPS, dtype=jnp.int32) <= step_index)[None, None, None, :]
    row_max = jnp.maximum(lax.optimization_barrier(jnp.max(jnp.where(cache_mask, cache_scores, -1e+30), axis=-1)), lax.optimization_barrier(jnp.max(jnp.where(fresh_mask, fresh_scores, -1e+30), axis=-1)))
    cache_exp = jnp.where(cache_mask, jnp.exp(cache_scores - row_max[..., None]), 0.0)
    fresh_exp = jnp.where(fresh_mask, jnp.exp(fresh_scores - row_max[..., None]), 0.0)
    row_total = lax.optimization_barrier(jnp.sum(cache_exp, axis=-1)) + lax.optimization_barrier(jnp.sum(fresh_exp, axis=-1))
    cache_probs = (cache_exp / row_total[..., None]).astype(jnp.bfloat16).astype(jnp.float32)
    fresh_probs = (fresh_exp / row_total[..., None]).astype(jnp.bfloat16).astype(jnp.float32)
    summed = jnp.einsum('rkgc,rckh->rkgh', cache_probs, values_cached) + jnp.einsum('rkgs,rskh->rkgh', fresh_probs, values_fresh)
    return summed.astype(jnp.bfloat16).reshape(rows_here, HEADS * HEAD)

def reference(hidden, norm_gain, gate_weights, routes, replica_pick, trainer_experts, hot_experts, replica_hot, w_gate, w_up, w_down, queries, key_cache, value_cache, new_keys, new_values, cache_lengths):
    device_ids = jnp.arange(N_EP, dtype=jnp.int32)
    expert_ids = jnp.arange(EXPERTS, dtype=jnp.int32)
    home_device = lax.optimization_barrier(jnp.sum(jnp.where(trainer_experts[None, :] == expert_ids[:, None], device_ids[None, :], 0), axis=1)).astype(jnp.int32)
    hosted = hot_experts[replica_hot]
    is_replica = (hosted[None, :] == expert_ids[:, None]).astype(jnp.int32)
    replica_order = (jnp.cumsum(is_replica, axis=1) * is_replica).astype(jnp.int32)
    copies = (1 + lax.optimization_barrier(jnp.sum(is_replica, axis=1))).astype(jnp.int32)
    slot_count = N_EP * SLOTS
    buffer_rows = slot_count * CAP
    blocks = TOKENS // TOK_DEV
    entries = TOK_DEV * TOP
    block_ids = jnp.broadcast_to(jnp.arange(blocks, dtype=jnp.int32)[:, None], (blocks, entries))
    token_of_entry = block_ids * TOK_DEV + jnp.arange(entries, dtype=jnp.int32)[None, :] // TOP
    mixed_steps = []
    context_steps = []
    for step_index in range(STEPS):
        normed = scaled_norm(hidden[step_index], norm_gain)
        weights_top = gate_weights[step_index]
        gates = (weights_top / lax.optimization_barrier(jnp.sum(weights_top, axis=-1, keepdims=True))).astype(jnp.bfloat16)
        chosen = routes[step_index].reshape(blocks, entries)
        replica_picks = replica_pick[step_index].reshape(blocks, entries)
        replica_index = (replica_picks % copies[chosen]).astype(jnp.int32)
        matches = replica_order[chosen] == replica_index[..., None]
        replica_device = lax.optimization_barrier(jnp.sum(jnp.where(matches, device_ids, 0), axis=-1)).astype(jnp.int32)
        target = jnp.where(replica_index == 0, home_device[chosen], replica_device)
        slot_index = (target * SLOTS + (replica_index > 0).astype(jnp.int32)).astype(jnp.int32)
        onehot = (slot_index[..., None] == jnp.arange(slot_count, dtype=jnp.int32)).astype(jnp.int32)
        slot_rank = (lax.optimization_barrier(jnp.sum(jnp.cumsum(onehot, axis=1) * onehot, axis=-1)) - 1).astype(jnp.int32)
        is_kept = slot_rank < CAP
        row_index = jnp.where(is_kept, slot_index * CAP + slot_rank, buffer_rows).astype(jnp.int32)
        token_table = jnp.zeros((blocks, buffer_rows), jnp.int32).at[block_ids, row_index].set(token_of_entry, mode='drop')
        gate_table = jnp.zeros((blocks, buffer_rows), jnp.float32).at[block_ids, row_index].set(gates.reshape(blocks, entries).astype(jnp.float32), mode='drop')
        token_table = token_table.reshape(blocks, slot_count, CAP).transpose(1, 0, 2).reshape(slot_count, blocks * CAP)
        gate_table = gate_table.reshape(blocks, slot_count, CAP).transpose(1, 0, 2).reshape(slot_count, blocks * CAP)

        def slot_body(summed, inputs):
            slot_tokens, slot_gates, slot_number = inputs
            owner_device = slot_number // SLOTS
            expert = jnp.where(slot_number % SLOTS == 0, trainer_experts[owner_device], hosted[owner_device])
            source = home_device[expert]
            rows_in = normed[slot_tokens]
            gate_part = jnp.dot(rows_in, w_gate[source], preferred_element_type=jnp.float32)
            up_part = jnp.dot(rows_in, w_up[source], preferred_element_type=jnp.float32)
            hidden_units = (jax.nn.silu(gate_part) * up_part).astype(jnp.bfloat16)
            result = jnp.dot(hidden_units, w_down[source], preferred_element_type=jnp.float32).astype(jnp.bfloat16)
            summed = summed.at[slot_tokens].add(slot_gates[:, None] * result.astype(jnp.float32))
            return (summed, None)
        summed, _ = lax.scan(slot_body, jnp.zeros((TOKENS, D), jnp.float32), (token_table, gate_table, jnp.arange(slot_count, dtype=jnp.int32)))
        mixed_steps.append((hidden[step_index].astype(jnp.float32) + summed).astype(jnp.bfloat16))
        block_inputs = (queries[step_index].reshape(blocks, TOK_DEV, HEADS * HEAD), key_cache.reshape(blocks, TOK_DEV, CACHE, KV_HEADS * HEAD), value_cache.reshape(blocks, TOK_DEV, CACHE, KV_HEADS * HEAD), jnp.swapaxes(new_keys, 0, 1).reshape(blocks, TOK_DEV, STEPS, KV_HEADS * HEAD), jnp.swapaxes(new_values, 0, 1).reshape(blocks, TOK_DEV, STEPS, KV_HEADS * HEAD), cache_lengths.reshape(blocks, TOK_DEV))
        attended = lax.map(lambda inputs: attend_block(inputs, step_index), block_inputs)
        context_steps.append(attended.reshape(TOKENS, HEADS * HEAD))
    return (jnp.stack(mixed_steps), jnp.stack(context_steps))
```

```python
import math

import jax
import jax.numpy as jnp
from jax import lax
from jax.sharding import PartitionSpec as P

HEADS = 32
KV_HEADS = 4
HEAD = 128
TOP = 8
CAP = 3
SLOTS = 2
LANES = 128
OUTER = 4
OUT_COLUMNS = 512
STEP_BYTES = 1 << 22

norm_epsilon = 1e-06


def scaled_norm(hidden_rows, norm_gain):
    values = hidden_rows.astype(jnp.float32)
    mean_square = jnp.mean(values * values, axis=-1, keepdims=True)
    return (values * lax.rsqrt(mean_square + norm_epsilon) * norm_gain.astype(jnp.float32)).astype(
        jnp.bfloat16
    )


def table_lookup(onehot_rows, table):
    return jnp.dot(onehot_rows, table, preferred_element_type=jnp.int32)


def attend(query_rows, key_cache, value_cache, new_keys, new_values, cache_lengths, step_index):
    rows_here = query_rows.shape[0]
    cache_len = key_cache.shape[1]
    steps_all = new_keys.shape[0]
    grouped = query_rows.reshape(rows_here, KV_HEADS, HEADS // KV_HEADS, HEAD)
    keys_cached = key_cache.reshape(rows_here, cache_len, KV_HEADS, HEAD)
    values_cached = value_cache.reshape(rows_here, cache_len, KV_HEADS, HEAD)
    keys_fresh = new_keys.reshape(steps_all, rows_here, KV_HEADS, HEAD)
    values_fresh = new_values.reshape(steps_all, rows_here, KV_HEADS, HEAD)
    score_scale = 1.0 / math.sqrt(HEAD)
    cache_scores = (
        jnp.einsum("rkgh,rckh->rkgc", grouped, keys_cached, preferred_element_type=jnp.float32)
        * score_scale
    )
    fresh_scores = (
        jnp.einsum("rkgh,srkh->rkgs", grouped, keys_fresh, preferred_element_type=jnp.float32)
        * score_scale
    )
    cache_mask = (jnp.arange(cache_len, dtype=jnp.int32)[None, :] < cache_lengths[:, None])[
        :, None, None, :
    ]
    fresh_mask = (jnp.arange(steps_all, dtype=jnp.int32) <= step_index)[None, None, None, :]
    row_max = jnp.maximum(
        jnp.max(jnp.where(cache_mask, cache_scores, -1e30), axis=-1),
        jnp.max(jnp.where(fresh_mask, fresh_scores, -1e30), axis=-1),
    )
    cache_exp = jnp.where(cache_mask, jnp.exp(cache_scores - row_max[..., None]), 0.0)
    fresh_exp = jnp.where(fresh_mask, jnp.exp(fresh_scores - row_max[..., None]), 0.0)
    row_total = jnp.sum(cache_exp, axis=-1) + jnp.sum(fresh_exp, axis=-1)
    cache_probs = (cache_exp / row_total[..., None]).astype(jnp.bfloat16)
    fresh_probs = (fresh_exp / row_total[..., None]).astype(jnp.bfloat16)
    summed = jnp.einsum(
        "rkgc,rckh->rkgh", cache_probs, values_cached, preferred_element_type=jnp.float32
    )
    summed = summed + jnp.einsum(
        "rkgs,srkh->rkgh", fresh_probs, values_fresh, preferred_element_type=jnp.float32
    )
    return summed.astype(jnp.bfloat16).reshape(rows_here, HEADS * HEAD)


def kept_gates(
    routes,
    replica_pick,
    gate_weights,
    expert_ids,
    device_ids,
    home_device,
    replica_order,
    copies,
):
    tokens_here = routes.shape[0]
    entries = tokens_here * TOP
    slot_total = device_ids.shape[0] * SLOTS
    gates = (gate_weights / jnp.sum(gate_weights, axis=-1, keepdims=True)).astype(jnp.bfloat16)
    chosen = routes.reshape(entries)
    replica_picks = replica_pick.reshape(entries)
    expert_onehot = (chosen[:, None] == expert_ids[None, :]).astype(jnp.int32)
    replica_index = replica_picks % table_lookup(expert_onehot, copies)
    order_rows = table_lookup(expert_onehot, replica_order)
    replica_device = jnp.sum(
        jnp.where(order_rows == replica_index[:, None], device_ids[None, :], 0), axis=1
    )
    target = jnp.where(replica_index == 0, table_lookup(expert_onehot, home_device), replica_device)
    slot_index = target * SLOTS + (replica_index > 0).astype(jnp.int32)
    slot_onehot = (
        slot_index[:, None] == jnp.arange(slot_total, dtype=jnp.int32)[None, :]
    ).astype(jnp.int32)
    slot_rank = jnp.sum(jnp.cumsum(slot_onehot, axis=0) * slot_onehot, axis=1) - 1
    kept = jnp.where(slot_rank < CAP, gates.reshape(entries).astype(jnp.float32), 0.0)
    spread = kept[:, None] * expert_onehot.astype(jnp.float32)
    return jnp.sum(spread.reshape(tokens_here, TOP, expert_ids.shape[0]), axis=1)


def roll_blocks(rows, start, count):
    width = rows.shape[1] // count
    twice = jnp.concatenate([rows, rows], axis=1)
    return lax.dynamic_slice_in_dim(twice, start * width, rows.shape[1], axis=1)


def swap(value, axis_size, stride):
    return lax.ppermute(value, "ep", [(i, i ^ stride) for i in range(axis_size)])


def pull(value, axis_size, inner, offset):
    outer = axis_size // inner
    return lax.ppermute(
        value,
        "ep",
        [
            (z * inner + r, (z - offset) % outer * inner + r)
            for z in range(outer)
            for r in range(inner)
        ],
    )


def gather_rows(rows, axis_size, inner):
    outer = axis_size // inner
    held = jnp.concatenate([rows] + [pull(rows, axis_size, inner, r) for r in range(1, outer)])
    stride = inner // 2
    while stride >= 1:
        held = jnp.concatenate([held, swap(held, axis_size, stride)])
        stride //= 2
    return held


def scatter_sum(values, axis_size, inner):
    outer = axis_size // inner
    stride = 1
    while stride < inner:
        half = values.shape[0] // 2
        values = values[:half] + swap(values[half:], axis_size, stride)
        stride *= 2
    rows = values.shape[0] // outer
    total = values[:rows]
    for r in range(1, outer):
        total = total + pull(values[r * rows : (r + 1) * rows], axis_size, inner, outer - r)
    return total


def one_step_at_a_time(hidden):
    return lax.axis_size("ep") * hidden.shape[1] * hidden.shape[2] * 2 > STEP_BYTES


def compute(
    hidden,
    norm_gain,
    gate_weights,
    routes,
    replica_pick,
    trainer_experts,
    hot_experts,
    replica_hot,
    w_gate,
    w_up,
    w_down,
    queries,
    key_cache,
    value_cache,
    new_keys,
    new_values,
    cache_lengths,
):
    ep_count = lax.axis_size("ep")
    dp_count = lax.axis_size("dp")
    my_device = lax.axis_index("ep")
    my_column = lax.axis_index("dp")
    inner = max(1, ep_count // OUTER)
    steps, _, width = hidden.shape
    block = width // dp_count

    def complete(shard):
        return [shard] + [
            lax.ppermute(shard, "dp", [(i, (i - s) % dp_count) for i in range(dp_count)])
            for s in range(1, dp_count)
        ]

    gate_parts = complete(w_gate[0])
    up_parts = complete(w_up[0])
    down_parts = complete(w_down[0])

    device_ids = jnp.arange(ep_count, dtype=jnp.int32)
    expert_count = trainer_experts.shape[0]
    expert_ids = jnp.arange(expert_count, dtype=jnp.int32)
    hot_ids = jnp.arange(hot_experts.shape[0], dtype=jnp.int32)
    home_device = jnp.sum(
        jnp.where(trainer_experts[None, :] == expert_ids[:, None], device_ids[None, :], 0), axis=1
    )
    hosted = jnp.sum(
        jnp.where(replica_hot[:, None] == hot_ids[None, :], hot_experts[None, :], 0), axis=1
    )
    is_replica = (hosted[None, :] == expert_ids[:, None]).astype(jnp.int32)
    replica_order = jnp.cumsum(is_replica, axis=1) * is_replica
    copies = 1 + jnp.sum(is_replica, axis=1)
    my_expert = jnp.sum(jnp.where(device_ids == my_device, trainer_experts, 0))
    lanes = -(-expert_count // LANES) * LANES

    gate_rest = jnp.concatenate(gate_parts[1:])
    up_rest = jnp.concatenate(up_parts[1:])
    span = max(1, OUT_COLUMNS // block)
    down_groups = [
        jnp.concatenate(down_parts[s : s + span], axis=1) for s in range(0, dp_count, span)
    ]
    lane = jnp.arange(lanes, dtype=jnp.int32)
    one_by_one = one_step_at_a_time(hidden)

    def prepare(step_index):
        normed = roll_blocks(scaled_norm(hidden[step_index], norm_gain), my_column, dp_count)
        kept = kept_gates(
            routes[step_index],
            replica_pick[step_index],
            gate_weights[step_index],
            expert_ids,
            device_ids,
            home_device,
            replica_order,
            copies,
        )
        kept = jnp.pad(kept.astype(jnp.bfloat16), ((0, 0), (0, lanes - expert_count)))
        return jnp.concatenate([normed, kept], axis=1)

    def process(packed):
        rows = gather_rows(packed, ep_count, inner)
        own = rows[:, :block]
        rest = rows[:, block:width]
        gate_part = jnp.dot(own, gate_parts[0], preferred_element_type=jnp.float32) + jnp.dot(
            rest, gate_rest, preferred_element_type=jnp.float32
        )
        up_part = jnp.dot(own, up_parts[0], preferred_element_type=jnp.float32) + jnp.dot(
            rest, up_rest, preferred_element_type=jnp.float32
        )
        units = (jax.nn.silu(gate_part) * up_part).astype(jnp.bfloat16)
        gate = jnp.sum(
            jnp.where(lane[None, :] == my_expert, rows[:, width:].astype(jnp.float32), 0.0),
            axis=1,
            keepdims=True,
        )
        blocks = []
        for s, down_part in enumerate(down_groups):
            if one_by_one and s:
                units, _ = lax.optimization_barrier((units, blocks[-1]))
            expert_out = jnp.dot(
                units, down_part, preferred_element_type=jnp.float32
            ).astype(jnp.bfloat16)
            weighted = gate * expert_out.astype(jnp.float32)
            blocks.append(scatter_sum(weighted, ep_count, inner))
        return jnp.concatenate(blocks, axis=1)

    if one_by_one:
        packed = jnp.stack([prepare(step_index) for step_index in range(steps)])
        sums = lax.map(lambda rows: process(rows), packed)
    else:
        sums = [process(prepare(step_index)) for step_index in range(steps)]

    context_steps = [
        attend(
            queries[step_index],
            key_cache,
            value_cache,
            new_keys,
            new_values,
            cache_lengths,
            step_index,
        )
        for step_index in range(steps)
    ]

    mixed_steps = []
    for step_index in range(steps):
        total = roll_blocks(sums[step_index], (dp_count - my_column) % dp_count, dp_count)
        mixed_steps.append(
            (hidden[step_index].astype(jnp.float32) + total).astype(jnp.bfloat16)
        )
    return (jnp.stack(mixed_steps), jnp.stack(context_steps))


def solution(mesh):
    return jax.shard_map(
        compute,
        mesh=mesh,
        in_specs=(
            P(None, ("ep", "dp"), None),
            P(),
            P(None, ("ep", "dp"), None),
            P(None, ("ep", "dp"), None),
            P(None, ("ep", "dp"), None),
            P(),
            P(),
            P(),
            P("ep", "dp", None),
            P("ep", "dp", None),
            P("ep", None, "dp"),
            P(None, ("ep", "dp"), None),
            P(("ep", "dp"), None, None),
            P(("ep", "dp"), None, None),
            P(None, ("ep", "dp"), None),
            P(None, ("ep", "dp"), None),
            P(("ep", "dp")),
        ),
        out_specs=(P(None, ("ep", "dp"), None), P(None, ("ep", "dp"), None)),
        check_vma=False,
    )
```

```python
import functools
import math

import jax
import jax.numpy as jnp
from jax import lax
from jax.experimental import pallas as pl
from jax.experimental.pallas import tpu as pltpu
from jax.sharding import PartitionSpec as P

HEADS = 32
KV_HEADS = 4
HEAD = 128
TOP = 8
CAP = 3
LANES = 128
OUTER = 4
OUT_COLUMNS = 512
RADIX = 64
STEP_BYTES = 1 << 22

norm_epsilon = 1e-06


def attend(query_rows, key_cache, value_cache, new_keys, new_values, cache_lengths, step_index):
    rows_here = query_rows.shape[0]
    cache_len = key_cache.shape[1]
    steps_all = new_keys.shape[0]
    grouped = query_rows.reshape(rows_here, KV_HEADS, HEADS // KV_HEADS, HEAD)
    keys_cached = key_cache.reshape(rows_here, cache_len, KV_HEADS, HEAD)
    values_cached = value_cache.reshape(rows_here, cache_len, KV_HEADS, HEAD)
    keys_fresh = new_keys.reshape(steps_all, rows_here, KV_HEADS, HEAD)
    values_fresh = new_values.reshape(steps_all, rows_here, KV_HEADS, HEAD)
    score_scale = 1.0 / math.sqrt(HEAD)
    cache_scores = (
        jnp.einsum("rkgh,rckh->rkgc", grouped, keys_cached, preferred_element_type=jnp.float32)
        * score_scale
    )
    fresh_scores = (
        jnp.einsum("rkgh,srkh->rkgs", grouped, keys_fresh, preferred_element_type=jnp.float32)
        * score_scale
    )
    cache_mask = (jnp.arange(cache_len, dtype=jnp.int32)[None, :] < cache_lengths[:, None])[
        :, None, None, :
    ]
    fresh_mask = (jnp.arange(steps_all, dtype=jnp.int32) <= step_index)[None, None, None, :]
    row_max = jnp.maximum(
        jnp.max(jnp.where(cache_mask, cache_scores, -1e30), axis=-1),
        jnp.max(jnp.where(fresh_mask, fresh_scores, -1e30), axis=-1),
    )
    cache_exp = jnp.where(cache_mask, jnp.exp(cache_scores - row_max[..., None]), 0.0)
    fresh_exp = jnp.where(fresh_mask, jnp.exp(fresh_scores - row_max[..., None]), 0.0)
    row_total = jnp.sum(cache_exp, axis=-1) + jnp.sum(fresh_exp, axis=-1)
    cache_probs = (cache_exp / row_total[..., None]).astype(jnp.bfloat16)
    fresh_probs = (fresh_exp / row_total[..., None]).astype(jnp.bfloat16)
    summed = jnp.einsum(
        "rkgc,rckh->rkgh", cache_probs, values_cached, preferred_element_type=jnp.float32
    )
    summed = summed + jnp.einsum(
        "rkgs,srkh->rkgh", fresh_probs, values_fresh, preferred_element_type=jnp.float32
    )
    return summed.astype(jnp.bfloat16).reshape(rows_here, HEADS * HEAD)


VMEM = pl.BlockSpec(memory_space=pltpu.VMEM)
SMEM = pl.BlockSpec(memory_space=pltpu.SMEM)


def exact_dot(left, right):
    return jnp.dot(
        left.astype(jnp.bfloat16), right.astype(jnp.bfloat16), preferred_element_type=jnp.float32
    )


def prepare_kernel(
    column_ref,
    hot_ref,
    trainer_ref,
    replica_hot_ref,
    gain_ref,
    hidden_ref,
    weights_ref,
    routes_ref,
    picks_ref,
    *packed_refs,
    dp_count,
):
    tokens = hidden_ref.shape[1]
    width = hidden_ref.shape[2]
    block = width // dp_count
    devices = trainer_ref.shape[1]
    entries = tokens * TOP
    trainer = trainer_ref[...]
    replica_hot = replica_hot_ref[...]
    hosted = jnp.zeros_like(replica_hot)
    for h in range(hot_ref.shape[0]):
        hosted = jnp.where(replica_hot == h, hot_ref[h], hosted)
    trainer = trainer.astype(jnp.float32)
    hosted = hosted.astype(jnp.float32)
    entry_row = lax.broadcasted_iota(jnp.int32, (entries, 1), 0)
    token_map = (
        lax.broadcasted_iota(jnp.int32, (entries, tokens), 1) == entry_row // TOP
    ).astype(jnp.float32)
    turn_map = (
        lax.broadcasted_iota(jnp.int32, (entries, TOP), 1) == entry_row % TOP
    ).astype(jnp.float32)
    earlier = (
        lax.broadcasted_iota(jnp.int32, (entries, entries), 1) <= entry_row
    ).astype(jnp.float32)
    ordered = (
        lax.broadcasted_iota(jnp.int32, (devices, devices), 0)
        <= lax.broadcasted_iota(jnp.int32, (devices, devices), 1)
    ).astype(jnp.float32)

    def as_column(table):
        return jnp.sum(exact_dot(token_map, table) * turn_map, axis=1, keepdims=True)

    gain = gain_ref[...].astype(jnp.float32)
    for step_index, packed_ref in enumerate(packed_refs):
        for s in range(dp_count):
            start = lax.rem(column_ref[0] + s, dp_count) * block
            if s == 0:
                values = hidden_ref[step_index].astype(jnp.float32)
                mean_square = jnp.mean(values * values, axis=-1, keepdims=True)
                scale = lax.rsqrt(mean_square + norm_epsilon)
            columns = pl.ds(pl.multiple_of(start, LANES), block)
            part = hidden_ref[step_index, :, columns].astype(jnp.float32)
            part = part * scale * gain_ref[:, columns].astype(jnp.float32)
            packed_ref[:, s * block : (s + 1) * block] = part.astype(jnp.bfloat16)
        top_weights = weights_ref[step_index]
        gates = (top_weights / jnp.sum(top_weights, axis=-1, keepdims=True)).astype(jnp.bfloat16)
        picks = picks_ref[step_index]
        pick_high = picks // RADIX
        pick_low = picks - pick_high * RADIX
        chosen = as_column(routes_ref[step_index].astype(jnp.float32))
        pick = as_column(pick_high.astype(jnp.float32)) * RADIX + as_column(
            pick_low.astype(jnp.float32)
        )
        gate = as_column(gates.astype(jnp.float32))
        at_home = (trainer == chosen).astype(jnp.float32)
        at_replica = (hosted == chosen).astype(jnp.float32)
        copies = 1.0 + jnp.sum(at_replica, axis=1, keepdims=True)
        order = exact_dot(at_replica, ordered) * at_replica
        replica_index = pick - copies * jnp.floor((pick + 0.5) / copies)
        first = (replica_index == 0.0).astype(jnp.float32)
        home_slot = at_home * first
        replica_slot = (order == replica_index).astype(jnp.float32) * (1.0 - first)
        home_rank = jnp.sum(
            exact_dot(earlier, home_slot) * home_slot, axis=1, keepdims=True
        )
        replica_rank = jnp.sum(
            exact_dot(earlier, replica_slot) * replica_slot, axis=1, keepdims=True
        )
        kept = jnp.where(home_rank + replica_rank <= CAP, gate, 0.0) * at_home
        spread = lax.dot_general(
            token_map.astype(jnp.bfloat16),
            kept.astype(jnp.bfloat16),
            (((0,), (0,)), ((), ())),
            preferred_element_type=jnp.float32,
        )
        packed_ref[:, width:] = jnp.zeros((tokens, packed_ref.shape[1] - width), jnp.bfloat16)
        packed_ref[:, width : width + devices] = spread.astype(jnp.bfloat16)


def join_kernel(*refs):
    out_ref = refs[-1]
    row = 0
    for ref in refs[:-1]:
        out_ref[row : row + ref.shape[0], :] = ref[...]
        row += ref.shape[0]


def join(parts):
    rows = sum(part.shape[0] for part in parts)
    return pl.pallas_call(
        join_kernel,
        out_shape=jax.ShapeDtypeStruct((rows, parts[0].shape[1]), parts[0].dtype),
        in_specs=[VMEM] * len(parts),
        out_specs=VMEM,
    )(*parts)


def own_gate(packed_gates, device):
    lane = lax.broadcasted_iota(jnp.int32, packed_gates.shape, 1)
    return jnp.sum(
        jnp.where(lane == device, packed_gates.astype(jnp.float32), 0.0), axis=1, keepdims=True
    )


def weighted_out(units, gate, down_ref):
    expert_out = jnp.dot(units, down_ref[...], preferred_element_type=jnp.float32)
    return gate * expert_out.astype(jnp.bfloat16).astype(jnp.float32)


def units_kernel(
    device_ref,
    here_ref,
    there_ref,
    gate_own_ref,
    gate_rest_ref,
    up_own_ref,
    up_rest_ref,
    down_ref,
    units_here_ref,
    units_there_ref,
    out_here_ref,
    out_there_ref,
    *,
    width,
):
    block = gate_own_ref.shape[0]

    def project(rows_ref, own_ref, rest_ref):
        return jnp.dot(
            rows_ref[:, :block], own_ref[...], preferred_element_type=jnp.float32
        ) + jnp.dot(rows_ref[:, block:width], rest_ref[...], preferred_element_type=jnp.float32)

    for rows_ref, units_ref, out_ref in (
        (there_ref, units_there_ref, out_there_ref),
        (here_ref, units_here_ref, out_here_ref),
    ):
        gate_part = project(rows_ref, gate_own_ref, gate_rest_ref)
        up_part = project(rows_ref, up_own_ref, up_rest_ref)
        units = (gate_part / (1.0 + jnp.exp(-gate_part)) * up_part).astype(jnp.bfloat16)
        units_ref[...] = units
        out_ref[...] = weighted_out(units, own_gate(rows_ref[:, width:], device_ref[0]), down_ref)


def out_kernel(
    device_ref,
    here_ref,
    there_ref,
    units_here_ref,
    units_there_ref,
    down_ref,
    out_here_ref,
    out_there_ref,
):
    for rows_ref, units_ref, out_ref in (
        (there_ref, units_there_ref, out_there_ref),
        (here_ref, units_here_ref, out_here_ref),
    ):
        out_ref[...] = weighted_out(
            units_ref[...], own_gate(rows_ref[...], device_ref[0]), down_ref
        )


def roll_blocks(rows, start, count):
    width = rows.shape[1] // count
    twice = jnp.concatenate([rows, rows], axis=1)
    return lax.dynamic_slice_in_dim(twice, start * width, rows.shape[1], axis=1)


def swap(value, axis_size, stride):
    return lax.ppermute(value, "ep", [(i, i ^ stride) for i in range(axis_size)])


def pull(value, axis_size, inner, offset):
    outer = axis_size // inner
    return lax.ppermute(
        value,
        "ep",
        [
            (z * inner + r, (z - offset) % outer * inner + r)
            for z in range(outer)
            for r in range(inner)
        ],
    )


def middle_strides(inner):
    stride = inner // 2
    while stride > 1:
        yield stride
        stride //= 2


def gather_rows(rows, axis_size, inner, inner_first):
    outer = axis_size // inner
    count = rows.shape[0]
    held = rows
    if not inner_first:
        pulled = [pull(held, axis_size, inner, r) for r in range(1, outer)]
        held = join([held] + pulled)
    for stride in middle_strides(inner):
        held = join([held, swap(held, axis_size, stride)])
    if inner_first:
        pulled = [held] + [pull(held, axis_size, inner, r) for r in range(1, outer)]
        held = join(
            [part[row : row + count] for row in range(0, held.shape[0], count) for part in pulled]
        )
    return held, swap(held, axis_size, 1)


def scatter_sum(keep, send, axis_size, inner):
    outer = axis_size // inner
    got = swap(send, axis_size, 1)
    for stride in reversed(list(middle_strides(inner))):
        half = keep.shape[0] // 2
        send = keep[half:] + got[half:]
        keep = keep[:half] + got[:half]
        got = swap(send, axis_size, stride)
    rows = keep.shape[0] // outer
    pulled = [
        pull(
            keep[r * rows : (r + 1) * rows] + got[r * rows : (r + 1) * rows],
            axis_size,
            inner,
            outer - r,
        )
        for r in range(1, outer)
    ]
    total = keep[:rows] + got[:rows]
    for part in pulled:
        total = total + part
    return total


def one_step_at_a_time(hidden):
    return lax.axis_size("ep") * hidden.shape[1] * hidden.shape[2] * 2 > STEP_BYTES


def compute(
    hidden,
    norm_gain,
    gate_weights,
    routes,
    replica_pick,
    trainer_experts,
    hot_experts,
    replica_hot,
    w_gate,
    w_up,
    w_down,
    queries,
    key_cache,
    value_cache,
    new_keys,
    new_values,
    cache_lengths,
):
    ep_count = lax.axis_size("ep")
    dp_count = lax.axis_size("dp")
    my_device = lax.axis_index("ep")
    my_column = lax.axis_index("dp")
    inner = max(1, ep_count // OUTER)
    steps, tokens_here, width = hidden.shape
    block = width // dp_count

    def complete(shard):
        return [shard] + [
            lax.ppermute(shard, "dp", [(i, (i - s) % dp_count) for i in range(dp_count)])
            for s in range(1, dp_count)
        ]

    gate_parts = complete(w_gate[0])
    up_parts = complete(w_up[0])
    down_parts = complete(w_down[0])

    lanes = -(-ep_count // LANES) * LANES
    packed_shape = jax.ShapeDtypeStruct((tokens_here, width + lanes), jnp.bfloat16)
    packed = pl.pallas_call(
        functools.partial(prepare_kernel, dp_count=dp_count),
        out_shape=[packed_shape] * steps,
        in_specs=[SMEM, SMEM] + [VMEM] * 7,
        out_specs=[VMEM] * steps,
    )(
        my_column.reshape(1),
        hot_experts,
        trainer_experts.reshape(1, ep_count),
        replica_hot.reshape(1, ep_count),
        norm_gain.reshape(1, width),
        hidden,
        gate_weights,
        routes,
        replica_pick,
    )
    gate_rest = jnp.concatenate(gate_parts[1:])
    up_rest = jnp.concatenate(up_parts[1:])
    one_by_one = one_step_at_a_time(hidden)
    span = max(1, OUT_COLUMNS // block)
    down_groups = [down_parts[0]] + [
        jnp.concatenate(down_parts[s : s + span], axis=1) for s in range(1, dp_count, span)
    ]
    device = my_device.reshape(1)

    def process(rows, inner_first):
        here, there = gather_rows(rows, ep_count, inner, inner_first)
        count = here.shape[0]
        hidden_units = w_gate.shape[2]

        def partial_sums(columns):
            return [jax.ShapeDtypeStruct((count, columns), jnp.float32)] * 2

        units_here, units_there, keep, send = pl.pallas_call(
            functools.partial(units_kernel, width=width),
            out_shape=[jax.ShapeDtypeStruct((count, hidden_units), jnp.bfloat16)] * 2
            + partial_sums(block),
            in_specs=[SMEM] + [VMEM] * 7,
            out_specs=[VMEM] * 4,
        )(
            device,
            here,
            there,
            gate_parts[0],
            gate_rest,
            up_parts[0],
            up_rest,
            down_groups[0],
        )
        gate_lanes = pl.BlockSpec((count, lanes), lambda i: (0, width // lanes))
        blocks = []
        for s, down_part in enumerate(down_groups):
            columns = down_part.shape[1]
            if s:
                if one_by_one:
                    units_here, _ = lax.optimization_barrier((units_here, blocks[-1]))
                keep, send = pl.pallas_call(
                    out_kernel,
                    grid=(1,),
                    out_shape=partial_sums(columns),
                    in_specs=[
                        SMEM,
                        gate_lanes,
                        gate_lanes,
                        pl.BlockSpec((count, hidden_units), lambda i: (0, 0)),
                        pl.BlockSpec((count, hidden_units), lambda i: (0, 0)),
                        pl.BlockSpec((hidden_units, columns), lambda i: (0, 0)),
                    ],
                    out_specs=[pl.BlockSpec((count, columns), lambda i: (0, 0))] * 2,
                )(device, here, there, units_here, units_there, down_part)
            blocks.append(scatter_sum(keep, send, ep_count, inner))
        return jnp.concatenate(blocks, axis=1)

    if one_by_one:
        sums = lax.map(lambda rows: process(rows, False), jnp.stack(packed))
    else:
        sums = [process(rows, step_index > 0) for step_index, rows in enumerate(packed)]

    context_steps = [
        attend(
            queries[step_index],
            key_cache,
            value_cache,
            new_keys,
            new_values,
            cache_lengths,
            step_index,
        )
        for step_index in range(steps)
    ]

    mixed_steps = []
    for step_index in range(steps):
        total = roll_blocks(sums[step_index], (dp_count - my_column) % dp_count, dp_count)
        mixed_steps.append(
            (hidden[step_index].astype(jnp.float32) + total).astype(jnp.bfloat16)
        )
    return (jnp.stack(mixed_steps), jnp.stack(context_steps))


def solution(mesh):
    return jax.shard_map(
        compute,
        mesh=mesh,
        in_specs=(
            P(None, ("ep", "dp"), None),
            P(),
            P(None, ("ep", "dp"), None),
            P(None, ("ep", "dp"), None),
            P(None, ("ep", "dp"), None),
            P(),
            P(),
            P(),
            P("ep", "dp", None),
            P("ep", "dp", None),
            P("ep", None, "dp"),
            P(None, ("ep", "dp"), None),
            P(("ep", "dp"), None, None),
            P(("ep", "dp"), None, None),
            P(None, ("ep", "dp"), None),
            P(None, ("ep", "dp"), None),
            P(("ep", "dp")),
        ),
        out_specs=(P(None, ("ep", "dp"), None), P(None, ("ep", "dp"), None)),
        check_vma=False,
    )
```
